32 devices in a mesh: depth: 4 (over y, core), row: 4 (over z), col: 2 (over x).
Axes of the slice: x: 2, y: 2, z: 4, core: 2. Of those that a mesh axis runs over, the one named last changes fastest.
Arguments:
- left_factor: bfloat16 [1792, 32, 512], P('depth', None, 'row'), may hold values from -6 to 6
- right_factor: bfloat16 [1792, 32, 512], P('depth', None, 'col'), may hold values from -6 to 6
- out_weight: bfloat16 [1024, 128], replicated, may hold values from -12 to 12
- pair_cotangent: bfloat16 [512, 512, 128], P(('row', 'depth'), 'col'), may hold values from -0.29882812 to 0.29882812
Outputs:
- left_grad: float32 [1792, 32, 512], P(('depth', 'col'), None, 'row')
- right_grad: float32 [1792, 32, 512], P(('depth', 'row'), None, 'col')
- weight_grad: float32 [1024, 128], P(('depth', 'row', 'col'))
The draws below stay inside these ranges and needn't reach their ends.
All inputs are finite; a program needn't handle non-finite values.
Results may differ from the reference program's by a relative error of at most 0.0075.
Values may be sent and summed in bfloat16 or wider, within the bound.
A program may use at most 320 MiB of HBM per device.

```python
import jax
import jax.numpy as jnp
from jax import lax

C = 32
P_SIZE = 128
TOK_ROW = 128
CC = 1024
S = 1792
N = 512


def block_scale(rng, dims, split, smallest, largest):
    gain = 1.0
    for axis_at, blocks in split:
        heights = jax.random.uniform(jax.random.fold_in(jax.random.fold_in(rng, 6), axis_at), (blocks,), jnp.float32, smallest / len(split), largest / len(split))
        gain = gain * jnp.repeat(jnp.exp(heights), dims[axis_at] // blocks).reshape((-1,) + (1,) * (len(dims) - 1 - axis_at))
    return gain


def bell_draw(key, shape, deviation, reach, shards=(), kind=jnp.bfloat16):
    factor_of = block_scale(key, shape, shards, -0.22, 0.18) if shards else 1.0
    entries = jax.random.normal(key, shape, jnp.float32) * deviation * factor_of
    return jnp.minimum(jnp.maximum(entries, -reach), reach).astype(kind)


def setup_inputs(seed: int = 0) -> dict:
    seeds = jax.random.split(jax.random.key(seed), 5)
    return {
        "left_factor": bell_draw(seeds[0], (S, C, N), 1.0, 6.0, ((0, 4), (2, 4))),
        "right_factor": bell_draw(seeds[1], (S, C, N), 1.0, 6.0, ((0, 4), (2, 2))),
        "out_weight": bell_draw(seeds[2], (CC, P_SIZE), 2.0, 12.0),
        "pair_cotangent": bell_draw(seeds[3], (N, N, P_SIZE), 0.05, 0.29882812, ((0, 16), (1, 2))),
    }


def reference(left_factor, right_factor, out_weight, pair_cotangent):
    seq_total = left_factor.shape[0]
    left_f = left_factor.astype(jnp.float32)
    right_f = right_factor.astype(jnp.float32)
    width = out_weight.shape[0]
    chans = left_factor.shape[1]
    pair_ch = out_weight.shape[1]
    tokens = left_factor.shape[2]
    blocks = tokens // TOK_ROW
    high = lax.Precision.HIGHEST

    def step(carry, block):
        wsum, rsum = carry
        first_row = (block * TOK_ROW).astype(jnp.int32)
        left_blk = lax.dynamic_slice_in_dim(left_f, first_row, TOK_ROW, 2)
        grad_blk = lax.dynamic_slice_in_dim(pair_cotangent, first_row, TOK_ROW, 0)
        outer = jnp.einsum('sci,sej->ijce', left_blk, right_f, precision=high) / seq_total
        outer = outer.reshape(TOK_ROW * tokens, width).astype(jnp.bfloat16)
        grad_two = grad_blk.reshape(TOK_ROW * tokens, pair_ch)
        delta = jnp.dot(grad_two, out_weight.T, preferred_element_type=jnp.float32).astype(jnp.bfloat16)
        wsum = wsum + jnp.dot(outer.T, grad_two, preferred_element_type=jnp.float32)
        delta_four = delta.astype(jnp.float32).reshape(TOK_ROW, tokens, chans, chans)
        left_blk_grad = jnp.einsum('ijce,sej->sci', delta_four, right_f, precision=high) / seq_total
        rsum = rsum + jnp.einsum('ijce,sci->sej', delta_four, left_blk, precision=high) / seq_total
        return (wsum, rsum), left_blk_grad

    start = (jnp.zeros((width, pair_ch), jnp.float32), jnp.zeros(right_f.shape, jnp.float32))
    (weight_grad, right_grad), pieces = lax.scan(step, start, jnp.arange(blocks, dtype=jnp.int32))
    left_grad = jnp.transpose(pieces, (1, 2, 0, 3)).reshape(seq_total, chans, tokens)
    return left_grad, right_grad, weight_grad
```

```python
import functools

import jax
import jax.numpy as jnp
from jax import lax
from jax.experimental import pallas as pl
from jax.experimental.pallas import tpu as pltpu
from jax.sharding import PartitionSpec as P

F32 = jnp.float32
BF16 = jnp.bfloat16
VMEM_CAP = 60 * 1024 * 1024


def params():
    return pltpu.CompilerParams(vmem_limit_bytes=VMEM_CAP)


def cost(flops, nbytes):
    return pl.CostEstimate(flops=flops, bytes_accessed=nbytes, transcendentals=0)


def outer_kernel(inv, at_ref, b_ref, o_ref):
    width = 512 if o_ref.shape[1] % 512 == 0 else o_ref.shape[1]
    for n in range(o_ref.shape[1] // width):
        cols = slice(n * width, (n + 1) * width)
        acc = jnp.dot(at_ref[...], b_ref[:, cols], preferred_element_type=F32)
        o_ref[:, cols] = (acc * inv).astype(BF16)


def outer_call(at, b2, inv, tm, tn):
    rows, seqs = at.shape
    cols = b2.shape[1]
    return pl.pallas_call(
        functools.partial(outer_kernel, inv),
        out_shape=jax.ShapeDtypeStruct((rows, cols), BF16),
        grid=(cols // tn, rows // tm),
        in_specs=[
            pl.BlockSpec((tm, seqs), lambda n, m: (m, 0)),
            pl.BlockSpec((seqs, tn), lambda n, m: (0, n)),
        ],
        out_specs=pl.BlockSpec((tm, tn), lambda n, m: (m, n)),
        compiler_params=params(),
        cost_estimate=cost(2 * rows * cols * seqs, 2 * rows * cols + 2 * seqs * (rows + cols)),
        name="outer",
    )(at, b2)


def delta_kernel(inv, chans, toks, w_ref, g_ref, a_ref, d_ref, r_ref, acc_ref):
    step = pl.program_id(0)
    here = g_ref.shape[0]
    eb = w_ref.shape[0] // chans

    def one(i, carry):
        d = lax.dot_general(
            w_ref[...], g_ref[i], (((1,), (1,)), ((), ())), preferred_element_type=F32
        ).astype(BF16)
        at = pl.multiple_of(i * chans, chans)
        for e in range(eb):
            d_ref[pl.ds(at, chans), e * toks:(e + 1) * toks] = d[e * chans:(e + 1) * chans]
        return carry

    lax.fori_loop(0, here, one, 0, unroll=8)

    @pl.when(step == 0)
    def _():
        acc_ref[...] = jnp.zeros_like(acc_ref)

    for e in range(eb):
        cols = slice(e * toks, (e + 1) * toks)
        acc_ref[:, cols] += jnp.dot(a_ref[...], d_ref[:, cols], preferred_element_type=F32)

    @pl.when(step == pl.num_programs(0) - 1)
    def _():
        r_ref[...] = (acc_ref[...] * inv).astype(BF16)


def delta_call(w_ec, g, a2, inv, chans, part, eb, ti):
    rows, toks, pair_ch = g.shape
    seqs = a2.shape[0]
    wide = eb * toks
    return pl.pallas_call(
        functools.partial(delta_kernel, inv, chans, toks),
        out_shape=(
            jax.ShapeDtypeStruct((rows * chans, wide), BF16),
            jax.ShapeDtypeStruct((seqs, wide), BF16),
        ),
        grid=(rows // ti,),
        in_specs=[
            pl.BlockSpec((eb * chans, pair_ch), lambda m: (part, 0)),
            pl.BlockSpec((ti, toks, pair_ch), lambda m: (m, 0, 0)),
            pl.BlockSpec((seqs, ti * chans), lambda m: (0, m)),
        ],
        out_specs=(
            pl.BlockSpec((ti * chans, wide), lambda m: (m, 0)),
            pl.BlockSpec((seqs, wide), lambda m: (0, 0)),
        ),
        scratch_shapes=[pltpu.VMEM((seqs, wide), F32)],
        compiler_params=params(),
        cost_estimate=cost(
            2 * rows * chans * wide * (seqs + 2 * pair_ch),
            2 * rows * (chans * wide + toks * pair_ch + chans * seqs),
        ),
        name=f"delta_right_{part}",
    )(w_ec, g, a2)


def left_kernel(inv, parts, b_ref, *refs):
    d_refs, o_ref = refs[:parts], refs[parts]
    wide = d_refs[0].shape[1]
    acc = None
    for k in range(parts):
        term = lax.dot_general(
            b_ref[:, k * wide:(k + 1) * wide],
            d_refs[k][...],
            (((1,), (1,)), ((), ())),
            preferred_element_type=F32,
        )
        acc = term if acc is None else acc + term
    o_ref[...] = acc * inv


def left_call(b2, ds, inv, tn):
    seqs = b2.shape[0]
    rows, wide = ds[0].shape
    parts = len(ds)
    return pl.pallas_call(
        functools.partial(left_kernel, inv, parts),
        out_shape=jax.ShapeDtypeStruct((seqs, rows), F32),
        grid=(rows // tn,),
        in_specs=[pl.BlockSpec((seqs, parts * wide), lambda m: (0, 0))]
        + [pl.BlockSpec((tn, wide), lambda m: (m, 0))] * parts,
        out_specs=pl.BlockSpec((seqs, tn), lambda m: (0, m)),
        compiler_params=params(),
        cost_estimate=cost(2 * seqs * rows * wide * parts, 2 * rows * wide * parts + 4 * seqs * rows),
        name="left",
    )(b2, *ds)


def weight_kernel(chans, o_ref, g_ref, w_ref):
    ti, toks, pair_ch = g_ref.shape
    width = w_ref.shape[0] // chans

    @pl.when(pl.program_id(0) == 0)
    def _():
        w_ref[...] = jnp.zeros_like(w_ref)

    group = 4
    eg = 8 if width % 8 == 0 else 1
    for i0 in range(0, ti, group):
        right = g_ref[i0:i0 + group].reshape(group * toks, pair_ch)
        for e0 in range(0, width, eg):
            left = jnp.concatenate(
                [
                    jnp.concatenate(
                        [
                            o_ref[i * chans:(i + 1) * chans, e * toks:(e + 1) * toks]
                            for i in range(i0, i0 + group)
                        ],
                        axis=1,
                    )
                    for e in range(e0, e0 + eg)
                ],
                axis=0,
            )
            w_ref[e0 * chans:(e0 + eg) * chans] += jnp.dot(left, right, preferred_element_type=F32)


def weight_call(outer, g, chans, ti):
    rows, toks, pair_ch = g.shape
    cols = outer.shape[1]
    width = cols // toks * chans
    return pl.pallas_call(
        functools.partial(weight_kernel, chans),
        out_shape=jax.ShapeDtypeStruct((width, pair_ch), F32),
        grid=(rows // ti,),
        in_specs=[
            pl.BlockSpec((ti * chans, cols), lambda m: (m, 0)),
            pl.BlockSpec((ti, toks, pair_ch), lambda m: (m, 0, 0)),
        ],
        out_specs=pl.BlockSpec((width, pair_ch), lambda m: (0, 0)),
        compiler_params=params(),
        cost_estimate=cost(4 * rows * toks * width * pair_ch, 2 * rows * chans * cols),
        name="weight",
    )(outer, g)


def fused_body(left_factor, right_factor, out_weight, pair_cotangent):
    seqs, chans, rows = left_factor.shape
    toks = right_factor.shape[2]
    pair_ch = out_weight.shape[1]
    inv = 1.0 / (seqs * lax.axis_size("depth"))
    n_col = lax.axis_size("col")
    parts = 4
    eb = chans // parts

    g = lax.all_gather(pair_cotangent, "depth", axis=0, tiled=True)
    a2 = jnp.transpose(left_factor, (0, 2, 1)).reshape(seqs, rows * chans)
    at = jnp.transpose(left_factor, (2, 1, 0)).reshape(rows * chans, seqs)
    b2 = right_factor.reshape(seqs, chans * toks)
    w_ec = jnp.transpose(out_weight.reshape(chans, chans, pair_ch), (1, 0, 2)).reshape(
        chans * chans, pair_ch
    )

    outer = outer_call(at, b2, inv, 16 * chans, eb * toks)
    g, outer = lax.optimization_barrier((g, outer))

    ds, rights = [], []
    for k in range(parts):
        d, r = delta_call(w_ec, g, a2, inv, chans, k, eb, 32)
        ds.append(d)
        rights.append(
            lax.psum_scatter(r.reshape(seqs, eb, toks), "row", scatter_dimension=0, tiled=True)
        )
    left = left_call(b2, ds, inv, 8 * chans)
    left, outer = lax.optimization_barrier((left, outer))
    left = jnp.transpose(left.reshape(seqs, rows, chans), (0, 2, 1))
    if n_col == 2:
        half = seqs // 2
        me = lax.axis_index("col")
        mine = lax.dynamic_slice_in_dim(left, me * half, half, 0)
        theirs = lax.dynamic_slice_in_dim(left, (1 - me) * half, half, 0).astype(BF16)
        got = lax.ppermute(theirs, "col", [(0, 1), (1, 0)])
        left_grad = mine + got.astype(F32)
    else:
        left_grad = lax.psum_scatter(left, "col", scatter_dimension=0, tiled=True)
    weight_acc = weight_call(outer, g, chans, 8)
    weight_acc = jnp.transpose(weight_acc.reshape(chans, chans, pair_ch), (1, 0, 2)).reshape(
        chans * chans, pair_ch
    )
    middle = lax.psum_scatter(weight_acc, ("depth", "row"), scatter_dimension=0, tiled=True)
    weight_grad = lax.psum_scatter(middle, "col", scatter_dimension=0, tiled=True)
    right_grad = jnp.concatenate(rights, axis=1).astype(F32)
    return left_grad, right_grad, weight_grad


def plain_body(left_factor, right_factor, out_weight, pair_cotangent):
    seq_total = left_factor.shape[0] * lax.axis_size("depth")
    chans = left_factor.shape[1]
    rows_here = left_factor.shape[2]
    cols_here = right_factor.shape[2]
    width = out_weight.shape[0]
    pair_ch = out_weight.shape[1]
    natural = jnp.einsum("sci,sej->ciej", left_factor, right_factor, preferred_element_type=F32) / seq_total
    outer = jnp.transpose(natural.astype(BF16), (1, 3, 0, 2)).reshape(rows_here * cols_here, width)
    piece = lax.all_gather(pair_cotangent, "depth", axis=0, tiled=True)
    grad_two = piece.reshape(rows_here * cols_here, pair_ch)
    delta = jnp.dot(grad_two, out_weight.T, preferred_element_type=F32).astype(BF16)
    weight_acc = jnp.dot(outer.T, grad_two, preferred_element_type=F32)
    delta_four = delta.reshape(rows_here, cols_here, chans, chans)
    left_part = jnp.einsum("ijce,sej->sci", delta_four, right_factor, preferred_element_type=F32) / seq_total
    right_part = jnp.einsum("ijce,sci->sej", delta_four, left_factor, preferred_element_type=F32) / seq_total
    left_grad = lax.psum_scatter(left_part, "col", scatter_dimension=0, tiled=True)
    right_grad = lax.psum_scatter(right_part, "row", scatter_dimension=0, tiled=True)
    middle = lax.psum_scatter(weight_acc, ("depth", "row"), scatter_dimension=0, tiled=True)
    weight_grad = lax.psum_scatter(middle, "col", scatter_dimension=0, tiled=True)
    return left_grad, right_grad, weight_grad


def body(left_factor, right_factor, out_weight, pair_cotangent):
    seqs, chans, rows = left_factor.shape
    toks = right_factor.shape[2]
    fits = toks % 128 == 0 and toks <= 256 and rows % 32 == 0 and chans == 32 and seqs <= 512
    run = fused_body if fits else plain_body
    return run(left_factor, right_factor, out_weight, pair_cotangent)


def solution(mesh):
    return jax.shard_map(
        body,
        mesh=mesh,
        in_specs=(
            P("depth", None, "row"),
            P("depth", None, "col"),
            P(),
            P(("row", "depth"), "col", None),
        ),
        out_specs=(
            P(("depth", "col"), None, "row"),
            P(("depth", "row"), None, "col"),
            P(("depth", "row", "col"), None),
        ),
        check_vma=False,
    )
```

```python
import functools

import jax
import jax.numpy as jnp
from jax import lax
from jax.experimental import pallas as pl
from jax.experimental.pallas import tpu as pltpu
from jax.sharding import PartitionSpec as P

F32 = jnp.float32
BF16 = jnp.bfloat16
VMEM_CAP = 60 * 1024 * 1024


def params():
    return pltpu.CompilerParams(vmem_limit_bytes=VMEM_CAP)


def cost(flops, nbytes):
    return pl.CostEstimate(flops=flops, bytes_accessed=nbytes, transcendentals=0)


def outer_kernel(inv, at_ref, b_ref, o_ref):
    width = 512 if o_ref.shape[1] % 512 == 0 else o_ref.shape[1]
    for n in range(o_ref.shape[1] // width):
        cols = slice(n * width, (n + 1) * width)
        acc = jnp.dot(at_ref[...], b_ref[:, cols], preferred_element_type=F32)
        o_ref[:, cols] = (acc * inv).astype(BF16)


def outer_call(at, b2, inv, tm, tn, part, cols):
    rows, seqs = at.shape
    first = part * cols // tn
    return pl.pallas_call(
        functools.partial(outer_kernel, inv),
        out_shape=jax.ShapeDtypeStruct((rows, cols), BF16),
        grid=(cols // tn, rows // tm),
        in_specs=[
            pl.BlockSpec((tm, seqs), lambda n, m: (m, 0)),
            pl.BlockSpec((seqs, tn), lambda n, m: (0, n + first)),
        ],
        out_specs=pl.BlockSpec((tm, tn), lambda n, m: (m, n)),
        compiler_params=params(),
        cost_estimate=cost(2 * rows * cols * seqs, 2 * rows * cols + 2 * seqs * (rows + cols)),
        name=f"outer_{part}",
    )(at, b2)


def delta_kernel(inv, chans, toks, w_ref, g_ref, a_ref, d_ref, r_ref, acc_ref):
    step = pl.program_id(0)
    here = g_ref.shape[0]
    eb = w_ref.shape[0] // chans

    def one(i, carry):
        d = lax.dot_general(
            w_ref[...], g_ref[i], (((1,), (1,)), ((), ())), preferred_element_type=F32
        ).astype(BF16)
        at = pl.multiple_of(i * chans, chans)
        for e in range(eb):
            d_ref[pl.ds(at, chans), e * toks:(e + 1) * toks] = d[e * chans:(e + 1) * chans]
        return carry

    lax.fori_loop(0, here, one, 0, unroll=8)

    @pl.when(step == 0)
    def _():
        acc_ref[...] = jnp.zeros_like(acc_ref)

    for e in range(eb):
        cols = slice(e * toks, (e + 1) * toks)
        acc_ref[:, cols] += jnp.dot(a_ref[...], d_ref[:, cols], preferred_element_type=F32)

    @pl.when(step == pl.num_programs(0) - 1)
    def _():
        r_ref[...] = (acc_ref[...] * inv).astype(BF16)


def delta_call(w_ec, g, a2, inv, chans, part, eb, ti):
    rows, toks, pair_ch = g.shape
    seqs = a2.shape[0]
    wide = eb * toks
    return pl.pallas_call(
        functools.partial(delta_kernel, inv, chans, toks),
        out_shape=(
            jax.ShapeDtypeStruct((rows * chans, wide), BF16),
            jax.ShapeDtypeStruct((seqs, wide), BF16),
        ),
        grid=(rows // ti,),
        in_specs=[
            pl.BlockSpec((eb * chans, pair_ch), lambda m: (part, 0)),
            pl.BlockSpec((ti, toks, pair_ch), lambda m: (m, 0, 0)),
            pl.BlockSpec((seqs, ti * chans), lambda m: (0, m)),
        ],
        out_specs=(
            pl.BlockSpec((ti * chans, wide), lambda m: (m, 0)),
            pl.BlockSpec((seqs, wide), lambda m: (0, 0)),
        ),
        scratch_shapes=[pltpu.VMEM((seqs, wide), F32)],
        compiler_params=params(),
        cost_estimate=cost(
            2 * rows * chans * wide * (seqs + 2 * pair_ch),
            2 * rows * (chans * wide + toks * pair_ch + chans * seqs),
        ),
        name=f"delta_right_{part}",
    )(w_ec, g, a2)


def left_kernel(inv, parts, b_ref, *refs):
    d_refs, o_ref = refs[:parts], refs[parts]
    wide = d_refs[0].shape[1]
    acc = None
    for k in range(parts):
        term = lax.dot_general(
            b_ref[:, k * wide:(k + 1) * wide],
            d_refs[k][...],
            (((1,), (1,)), ((), ())),
            preferred_element_type=F32,
        )
        acc = term if acc is None else acc + term
    o_ref[...] = (acc * inv).astype(BF16)


def left_call(b2, ds, inv, tn):
    seqs = b2.shape[0]
    rows, wide = ds[0].shape
    parts = len(ds)
    return pl.pallas_call(
        functools.partial(left_kernel, inv, parts),
        out_shape=jax.ShapeDtypeStruct((seqs, rows), BF16),
        grid=(rows // tn,),
        in_specs=[pl.BlockSpec((seqs, parts * wide), lambda m: (0, 0))]
        + [pl.BlockSpec((tn, wide), lambda m: (m, 0))] * parts,
        out_specs=pl.BlockSpec((seqs, tn), lambda m: (0, m)),
        compiler_params=params(),
        cost_estimate=cost(2 * seqs * rows * wide * parts, 2 * rows * wide * parts + 4 * seqs * rows),
        name="left",
    )(b2, *ds)


def weight_kernel(chans, *refs):
    o_refs, g_ref, w_ref = refs[:-2], refs[-2], refs[-1]
    ti, toks, pair_ch = g_ref.shape
    per = o_refs[0].shape[1] // toks

    @pl.when(pl.program_id(0) == 0)
    def _():
        w_ref[...] = jnp.zeros_like(w_ref)

    group = 4
    eg = 8 if per % 8 == 0 else 1
    for i0 in range(0, ti, group):
        right = g_ref[i0:i0 + group].reshape(group * toks, pair_ch)
        for h, o_ref in enumerate(o_refs):
            for e0 in range(0, per, eg):
                left = jnp.concatenate(
                    [
                        jnp.concatenate(
                            [
                                o_ref[i * chans:(i + 1) * chans, e * toks:(e + 1) * toks]
                                for i in range(i0, i0 + group)
                            ],
                            axis=1,
                        )
                        for e in range(e0, e0 + eg)
                    ],
                    axis=0,
                )
                at = (h * per + e0) * chans
                w_ref[at:at + eg * chans] += jnp.dot(left, right, preferred_element_type=F32)


def weight_call(outers, g, chans, ti):
    rows, toks, pair_ch = g.shape
    cols = outers[0].shape[1]
    width = cols * len(outers) // toks * chans
    return pl.pallas_call(
        functools.partial(weight_kernel, chans),
        out_shape=jax.ShapeDtypeStruct((width, pair_ch), F32),
        grid=(rows // ti,),
        in_specs=[pl.BlockSpec((ti * chans, cols), lambda m: (m, 0))] * len(outers)
        + [pl.BlockSpec((ti, toks, pair_ch), lambda m: (m, 0, 0))],
        out_specs=pl.BlockSpec((width, pair_ch), lambda m: (0, 0)),
        compiler_params=params(),
        cost_estimate=cost(4 * rows * toks * width * pair_ch, 2 * rows * toks * width),
        name="weight",
    )(*outers, g)


def fused_body(left_factor, right_factor, out_weight, pair_cotangent):
    seqs, chans, rows = left_factor.shape
    toks = right_factor.shape[2]
    pair_ch = out_weight.shape[1]
    inv = 1.0 / (seqs * lax.axis_size("depth"))
    n_col = lax.axis_size("col")
    parts = 4
    eb = chans // parts

    g = lax.all_gather(pair_cotangent, "depth", axis=0, tiled=True)
    a2 = jnp.transpose(left_factor, (0, 2, 1)).reshape(seqs, rows * chans)
    at = jnp.transpose(left_factor, (2, 1, 0)).reshape(rows * chans, seqs)
    b2 = right_factor.reshape(seqs, chans * toks)
    w_ec = jnp.transpose(out_weight.reshape(chans, chans, pair_ch), (1, 0, 2)).reshape(
        chans * chans, pair_ch
    )

    half_cols = b2.shape[1] // 2
    outer_a = outer_call(at, b2, inv, 16 * chans, eb * toks, 0, half_cols)
    g, outer_a = lax.optimization_barrier((g, outer_a))

    ds, rights = [], []
    for k in range(parts):
        d, r = delta_call(w_ec, g, a2, inv, chans, k, eb, 32)
        ds.append(d)
        r, g = lax.optimization_barrier((r.reshape(seqs, eb, toks), g))
        rights.append(lax.psum_scatter(r, "row", scatter_dimension=0, tiled=True))
    left = left_call(b2, ds, inv, 8 * chans)
    left = jnp.transpose(left.reshape(seqs, rows, chans), (0, 2, 1))
    left, at, b2 = lax.optimization_barrier((left, at, b2))
    if n_col == 2:
        half = seqs // 2
        me = lax.axis_index("col")
        mine = lax.dynamic_slice_in_dim(left, me * half, half, 0)
        theirs = lax.dynamic_slice_in_dim(left, (1 - me) * half, half, 0)
        theirs, at, b2 = lax.optimization_barrier((theirs, at, b2))
        got = lax.ppermute(theirs, "col", [(0, 1), (1, 0)])
        left_grad = mine.astype(F32) + got.astype(F32)
    else:
        left_grad = lax.psum_scatter(left, "col", scatter_dimension=0, tiled=True).astype(F32)
    outer_b = outer_call(at, b2, inv, 16 * chans, eb * toks, 1, half_cols)
    weight_acc = weight_call((outer_a, outer_b), g, chans, 4)
    weight_acc = jnp.transpose(weight_acc.reshape(chans, chans, pair_ch), (1, 0, 2)).reshape(
        chans * chans, pair_ch
    )
    weight_acc, *rights = lax.optimization_barrier((weight_acc, *rights))
    middle = lax.psum_scatter(weight_acc, ("depth", "row"), scatter_dimension=0, tiled=True)
    weight_grad = lax.psum_scatter(middle, "col", scatter_dimension=0, tiled=True)
    right_grad = jnp.concatenate(rights, axis=1).astype(F32)
    return left_grad, right_grad, weight_grad


def plain_body(left_factor, right_factor, out_weight, pair_cotangent):
    seq_total = left_factor.shape[0] * lax.axis_size("depth")
    chans = left_factor.shape[1]
    rows_here = left_factor.shape[2]
    cols_here = right_factor.shape[2]
    width = out_weight.shape[0]
    pair_ch = out_weight.shape[1]
    natural = jnp.einsum("sci,sej->ciej", left_factor, right_factor, preferred_element_type=F32) / seq_total
    outer = jnp.transpose(natural.astype(BF16), (1, 3, 0, 2)).reshape(rows_here * cols_here, width)
    piece = lax.all_gather(pair_cotangent, "depth", axis=0, tiled=True)
    grad_two = piece.reshape(rows_here * cols_here, pair_ch)
    delta = jnp.dot(grad_two, out_weight.T, preferred_element_type=F32).astype(BF16)
    weight_acc = jnp.dot(outer.T, grad_two, preferred_element_type=F32)
    delta_four = delta.reshape(rows_here, cols_here, chans, chans)
    left_part = jnp.einsum("ijce,sej->sci", delta_four, right_factor, preferred_element_type=F32) / seq_total
    right_part = jnp.einsum("ijce,sci->sej", delta_four, left_factor, preferred_element_type=F32) / seq_total
    left_grad = lax.psum_scatter(left_part, "col", scatter_dimension=0, tiled=True)
    right_grad = lax.psum_scatter(right_part, "row", scatter_dimension=0, tiled=True)
    middle = lax.psum_scatter(weight_acc, ("depth", "row"), scatter_dimension=0, tiled=True)
    weight_grad = lax.psum_scatter(middle, "col", scatter_dimension=0, tiled=True)
    return left_grad, right_grad, weight_grad


def body(left_factor, right_factor, out_weight, pair_cotangent):
    seqs, chans, rows = left_factor.shape
    toks = right_factor.shape[2]
    fits = toks % 128 == 0 and toks <= 256 and rows % 32 == 0 and chans == 32 and seqs <= 512
    run = fused_body if fits else plain_body
    return run(left_factor, right_factor, out_weight, pair_cotangent)


def solution(mesh):
    return jax.shard_map(
        body,
        mesh=mesh,
        in_specs=(
            P("depth", None, "row"),
            P("depth", None, "col"),
            P(),
            P(("row", "depth"), "col", None),
        ),
        out_specs=(
            P(("depth", "col"), None, "row"),
            P(("depth", "row"), None, "col"),
            P(("depth", "row", "col"), None),
        ),
        check_vma=False,
    )
```

```python
import functools

import jax
import jax.numpy as jnp
from jax import lax
from jax.experimental import pallas as pl
from jax.experimental.pallas import tpu as pltpu
from jax.sharding import PartitionSpec as P

F32 = jnp.float32
BF16 = jnp.bfloat16
VMEM_CAP = 60 * 1024 * 1024


def params():
    return pltpu.CompilerParams(vmem_limit_bytes=VMEM_CAP)


def cost(flops, nbytes):
    return pl.CostEstimate(flops=flops, bytes_accessed=nbytes, transcendentals=0)


def outer_kernel(inv, at_ref, b_ref, o_ref):
    width = 512 if o_ref.shape[1] % 512 == 0 else o_ref.shape[1]
    for n in range(o_ref.shape[1] // width):
        cols = slice(n * width, (n + 1) * width)
        acc = jnp.dot(at_ref[...], b_ref[:, cols], preferred_element_type=F32)
        o_ref[:, cols] = (acc * inv).astype(BF16)


def outer_call(at, b2, inv, tm, tn, part, cols):
    rows, seqs = at.shape
    first = part * cols // tn
    return pl.pallas_call(
        functools.partial(outer_kernel, inv),
        out_shape=jax.ShapeDtypeStruct((rows, cols), BF16),
        grid=(cols // tn, rows // tm),
        in_specs=[
            pl.BlockSpec((tm, seqs), lambda n, m: (m, 0)),
            pl.BlockSpec((seqs, tn), lambda n, m: (0, n + first)),
        ],
        out_specs=pl.BlockSpec((tm, tn), lambda n, m: (m, n)),
        compiler_params=params(),
        cost_estimate=cost(2 * rows * cols * seqs, 2 * rows * cols + 2 * seqs * (rows + cols)),
        name=f"outer_{part}",
    )(at, b2)


def delta_kernel(inv, chans, toks, w_ref, g_ref, a_ref, d_ref, r_ref, acc_ref):
    step = pl.program_id(0)
    here = g_ref.shape[0]
    eb = w_ref.shape[0] // chans

    def one(i, carry):
        d = lax.dot_general(
            w_ref[...], g_ref[i], (((1,), (1,)), ((), ())), preferred_element_type=F32
        ).astype(BF16)
        at = pl.multiple_of(i * chans, chans)
        for e in range(eb):
            d_ref[pl.ds(at, chans), e * toks:(e + 1) * toks] = d[e * chans:(e + 1) * chans]
        return carry

    lax.fori_loop(0, here, one, 0, unroll=8)

    @pl.when(step == 0)
    def _():
        acc_ref[...] = jnp.zeros_like(acc_ref)

    for e in range(eb):
        cols = slice(e * toks, (e + 1) * toks)
        acc_ref[:, cols] += jnp.dot(a_ref[...], d_ref[:, cols], preferred_element_type=F32)

    @pl.when(step == pl.num_programs(0) - 1)
    def _():
        r_ref[...] = (acc_ref[...] * inv).astype(BF16)


def delta_call(w_ec, g, a2, inv, chans, part, eb, ti):
    rows, toks, pair_ch = g.shape
    seqs = a2.shape[0]
    wide = eb * toks
    return pl.pallas_call(
        functools.partial(delta_kernel, inv, chans, toks),
        out_shape=(
            jax.ShapeDtypeStruct((rows * chans, wide), BF16),
            jax.ShapeDtypeStruct((seqs, wide), BF16),
        ),
        grid=(rows // ti,),
        in_specs=[
            pl.BlockSpec((eb * chans, pair_ch), lambda m: (part, 0)),
            pl.BlockSpec((ti, toks, pair_ch), lambda m: (m, 0, 0)),
            pl.BlockSpec((seqs, ti * chans), lambda m: (0, m)),
        ],
        out_specs=(
            pl.BlockSpec((ti * chans, wide), lambda m: (m, 0)),
            pl.BlockSpec((seqs, wide), lambda m: (0, 0)),
        ),
        scratch_shapes=[pltpu.VMEM((seqs, wide), F32)],
        compiler_params=params(),
        cost_estimate=cost(
            2 * rows * chans * wide * (seqs + 2 * pair_ch),
            2 * rows * (chans * wide + toks * pair_ch + chans * seqs),
        ),
        name=f"delta_right_{part}",
    )(w_ec, g, a2)


def left_kernel(inv, parts, b_ref, *refs):
    d_refs, o_ref = refs[:parts], refs[parts]
    wide = d_refs[0].shape[1]
    acc = None
    for k in range(parts):
        term = lax.dot_general(
            b_ref[:, k * wide:(k + 1) * wide],
            d_refs[k][...],
            (((1,), (1,)), ((), ())),
            preferred_element_type=F32,
        )
        acc = term if acc is None else acc + term
    o_ref[...] = (acc * inv).astype(BF16)


def left_call(b2, ds, inv, tn):
    seqs = b2.shape[0]
    rows, wide = ds[0].shape
    parts = len(ds)
    return pl.pallas_call(
        functools.partial(left_kernel, inv, parts),
        out_shape=jax.ShapeDtypeStruct((seqs, rows), BF16),
        grid=(rows // tn,),
        in_specs=[pl.BlockSpec((seqs, parts * wide), lambda m: (0, 0))]
        + [pl.BlockSpec((tn, wide), lambda m: (m, 0))] * parts,
        out_specs=pl.BlockSpec((seqs, tn), lambda m: (0, m)),
        compiler_params=params(),
        cost_estimate=cost(2 * seqs * rows * wide * parts, 2 * rows * wide * parts + 4 * seqs * rows),
        name="left",
    )(b2, *ds)


def weight_kernel(chans, *refs):
    o_refs, g_ref, w_ref = refs[:-2], refs[-2], refs[-1]
    ti, toks, pair_ch = g_ref.shape
    per = o_refs[0].shape[1] // toks

    @pl.when(pl.program_id(0) == 0)
    def _():
        w_ref[...] = jnp.zeros_like(w_ref)

    group = 4
    eg = 8 if per % 8 == 0 else 1

    def one(k, carry):
        first = pl.multiple_of(k * group, group)
        right = g_ref[pl.ds(first, group)].reshape(group * toks, pair_ch)
        for h, o_ref in enumerate(o_refs):
            for e0 in range(0, per, eg):
                left = jnp.concatenate(
                    [
                        jnp.concatenate(
                            [
                                o_ref[
                                    pl.ds(pl.multiple_of((first + i) * chans, chans), chans),
                                    e * toks:(e + 1) * toks,
                                ]
                                for i in range(group)
                            ],
                            axis=1,
                        )
                        for e in range(e0, e0 + eg)
                    ],
                    axis=0,
                )
                at = (h * per + e0) * chans
                w_ref[at:at + eg * chans] += jnp.dot(left, right, preferred_element_type=F32)
        return carry

    lax.fori_loop(0, ti // group, one, 0)


def weight_call(outers, g, chans, ti):
    rows, toks, pair_ch = g.shape
    cols = outers[0].shape[1]
    width = cols * len(outers) // toks * chans
    return pl.pallas_call(
        functools.partial(weight_kernel, chans),
        out_shape=jax.ShapeDtypeStruct((width, pair_ch), F32),
        grid=(rows // ti,),
        in_specs=[pl.BlockSpec((ti * chans, cols), lambda m: (m, 0))] * len(outers)
        + [pl.BlockSpec((ti, toks, pair_ch), lambda m: (m, 0, 0))],
        out_specs=pl.BlockSpec((width, pair_ch), lambda m: (0, 0)),
        compiler_params=params(),
        cost_estimate=cost(4 * rows * toks * width * pair_ch, 2 * rows * toks * width),
        name="weight",
    )(*outers, g)


def fused_body(left_factor, right_factor, out_weight, pair_cotangent):
    seqs, chans, rows = left_factor.shape
    toks = right_factor.shape[2]
    pair_ch = out_weight.shape[1]
    inv = 1.0 / (seqs * lax.axis_size("depth"))
    n_col = lax.axis_size("col")
    parts = 4
    eb = chans // parts

    g = lax.all_gather(pair_cotangent, "depth", axis=0, tiled=True)
    a2 = jnp.transpose(left_factor, (0, 2, 1)).reshape(seqs, rows * chans)
    at = jnp.transpose(left_factor, (2, 1, 0)).reshape(rows * chans, seqs)
    b2 = right_factor.reshape(seqs, chans * toks)
    w_ec = jnp.transpose(out_weight.reshape(chans, chans, pair_ch), (1, 0, 2)).reshape(
        chans * chans, pair_ch
    )

    half_cols = b2.shape[1] // 2
    outer_a = outer_call(at, b2, inv, 16 * chans, eb * toks, 0, half_cols)
    g, outer_a = lax.optimization_barrier((g, outer_a))

    ds, rights = [], []
    for k in range(parts):
        d, r = delta_call(w_ec, g, a2, inv, chans, k, eb, 32)
        ds.append(d)
        r, g = lax.optimization_barrier((r, g))
        rights.append(lax.psum_scatter(r, "row", scatter_dimension=0, tiled=True))
    left = left_call(b2, ds, inv, 8 * chans)
    left, at, b2 = lax.optimization_barrier((left, at, b2))
    if n_col == 2:
        half = seqs // 2
        me = lax.axis_index("col")
        mine = lax.dynamic_slice_in_dim(left, me * half, half, 0)
        theirs = lax.dynamic_slice_in_dim(left, (1 - me) * half, half, 0)
        theirs, at, b2 = lax.optimization_barrier((theirs, at, b2))
        got = lax.ppermute(theirs, "col", [(0, 1), (1, 0)])
        left_grad = mine.astype(F32) + got.astype(F32)
    else:
        left_grad = lax.psum_scatter(left, "col", scatter_dimension=0, tiled=True).astype(F32)
    left_grad = jnp.transpose(left_grad.reshape(-1, rows, chans), (0, 2, 1))
    outer_b = outer_call(at, b2, inv, 16 * chans, eb * toks, 1, half_cols)
    weight_acc = weight_call((outer_a, outer_b), g, chans, 8)
    weight_acc = jnp.transpose(weight_acc.reshape(chans, chans, pair_ch), (1, 0, 2)).reshape(
        chans * chans, pair_ch
    )
    axes = ("depth", "row", "col")
    count = lax.axis_size(axes)
    pieces = weight_acc.reshape(count, chans * chans // count, pair_ch)
    pieces = lax.all_to_all(pieces, axes, split_axis=0, concat_axis=0, tiled=True)
    weight_grad = jnp.sum(pieces, axis=0)
    rights = [r.reshape(-1, eb, toks) for r in rights]
    right_grad = jnp.concatenate(rights, axis=1).astype(F32)
    return left_grad, right_grad, weight_grad


def plain_body(left_factor, right_factor, out_weight, pair_cotangent):
    seq_total = left_factor.shape[0] * lax.axis_size("depth")
    chans = left_factor.shape[1]
    rows_here = left_factor.shape[2]
    cols_here = right_factor.shape[2]
    width = out_weight.shape[0]
    pair_ch = out_weight.shape[1]
    natural = jnp.einsum("sci,sej->ciej", left_factor, right_factor, preferred_element_type=F32) / seq_total
    outer = jnp.transpose(natural.astype(BF16), (1, 3, 0, 2)).reshape(rows_here * cols_here, width)
    piece = lax.all_gather(pair_cotangent, "depth", axis=0, tiled=True)
    grad_two = piece.reshape(rows_here * cols_here, pair_ch)
    delta = jnp.dot(grad_two, out_weight.T, preferred_element_type=F32).astype(BF16)
    weight_acc = jnp.dot(outer.T, grad_two, preferred_element_type=F32)
    delta_four = delta.reshape(rows_here, cols_here, chans, chans)
    left_part = jnp.einsum("ijce,sej->sci", delta_four, right_factor, preferred_element_type=F32) / seq_total
    right_part = jnp.einsum("ijce,sci->sej", delta_four, left_factor, preferred_element_type=F32) / seq_total
    left_grad = lax.psum_scatter(left_part, "col", scatter_dimension=0, tiled=True)
    right_grad = lax.psum_scatter(right_part, "row", scatter_dimension=0, tiled=True)
    middle = lax.psum_scatter(weight_acc, ("depth", "row"), scatter_dimension=0, tiled=True)
    weight_grad = lax.psum_scatter(middle, "col", scatter_dimension=0, tiled=True)
    return left_grad, right_grad, weight_grad


def body(left_factor, right_factor, out_weight, pair_cotangent):
    seqs, chans, rows = left_factor.shape
    toks = right_factor.shape[2]
    fits = toks % 128 == 0 and toks <= 256 and rows % 32 == 0 and chans == 32 and seqs <= 512
    run = fused_body if fits else plain_body
    return run(left_factor, right_factor, out_weight, pair_cotangent)


def solution(mesh):
    return jax.shard_map(
        body,
        mesh=mesh,
        in_specs=(
            P("depth", None, "row"),
            P("depth", None, "col"),
            P(),
            P(("row", "depth"), "col", None),
        ),
        out_specs=(
            P(("depth", "col"), None, "row"),
            P(("depth", "row"), None, "col"),
            P(("depth", "row", "col"), None),
        ),
        check_vma=False,
    )
```

```python
import functools

import jax
import jax.numpy as jnp
from jax import lax
from jax.experimental import pallas as pl
from jax.experimental.pallas import tpu as pltpu
from jax.sharding import PartitionSpec as P

F32 = jnp.float32
BF16 = jnp.bfloat16
VMEM_CAP = 60 * 1024 * 1024


def params():
    return pltpu.CompilerParams(vmem_limit_bytes=VMEM_CAP)


def cost(flops, nbytes):
    return pl.CostEstimate(flops=flops, bytes_accessed=nbytes, transcendentals=0)


def outer_kernel(inv, at_ref, b_ref, o_ref):
    width = 512 if o_ref.shape[1] % 512 == 0 else o_ref.shape[1]
    for n in range(o_ref.shape[1] // width):
        cols = slice(n * width, (n + 1) * width)
        acc = jnp.dot(at_ref[...], b_ref[:, cols], preferred_element_type=F32)
        o_ref[:, cols] = (acc * inv).astype(BF16)


def outer_call(at, b2, inv, tm, tn, part, cols):
    rows, seqs = at.shape
    first = part * cols // tn
    return pl.pallas_call(
        functools.partial(outer_kernel, inv),
        out_shape=jax.ShapeDtypeStruct((rows, cols), BF16),
        grid=(cols // tn, rows // tm),
        in_specs=[
            pl.BlockSpec((tm, seqs), lambda n, m: (m, 0)),
            pl.BlockSpec((seqs, tn), lambda n, m: (0, n + first)),
        ],
        out_specs=pl.BlockSpec((tm, tn), lambda n, m: (m, n)),
        compiler_params=params(),
        cost_estimate=cost(2 * rows * cols * seqs, 2 * rows * cols + 2 * seqs * (rows + cols)),
        name=f"outer_{part}",
    )(at, b2)


def delta_kernel(inv, chans, toks, w_ref, g_ref, a_ref, d_ref, r_ref, acc_ref):
    step = pl.program_id(0)
    here = g_ref.shape[0]
    eb = w_ref.shape[0] // chans

    def one(i, carry):
        d = lax.dot_general(
            w_ref[...], g_ref[i], (((1,), (1,)), ((), ())), preferred_element_type=F32
        ).astype(BF16)
        at = pl.multiple_of(i * chans, chans)
        for e in range(eb):
            d_ref[pl.ds(at, chans), e * toks:(e + 1) * toks] = d[e * chans:(e + 1) * chans]
        return carry

    lax.fori_loop(0, here, one, 0, unroll=8)

    @pl.when(step == 0)
    def _():
        acc_ref[...] = jnp.zeros_like(acc_ref)

    for e in range(eb):
        cols = slice(e * toks, (e + 1) * toks)
        acc_ref[:, cols] += jnp.dot(a_ref[...], d_ref[:, cols], preferred_element_type=F32)

    @pl.when(step == pl.num_programs(0) - 1)
    def _():
        r_ref[...] = (acc_ref[...] * inv).astype(BF16)


def delta_call(w_ec, g, a2, inv, chans, part, eb, ti):
    rows, toks, pair_ch = g.shape
    seqs = a2.shape[0]
    wide = eb * toks
    return pl.pallas_call(
        functools.partial(delta_kernel, inv, chans, toks),
        out_shape=(
            jax.ShapeDtypeStruct((rows * chans, wide), BF16),
            jax.ShapeDtypeStruct((seqs, wide), BF16),
        ),
        grid=(rows // ti,),
        in_specs=[
            pl.BlockSpec((eb * chans, pair_ch), lambda m: (part, 0)),
            pl.BlockSpec((ti, toks, pair_ch), lambda m: (m, 0, 0)),
            pl.BlockSpec((seqs, ti * chans), lambda m: (0, m)),
        ],
        out_specs=(
            pl.BlockSpec((ti * chans, wide), lambda m: (m, 0)),
            pl.BlockSpec((seqs, wide), lambda m: (0, 0)),
        ),
        scratch_shapes=[pltpu.VMEM((seqs, wide), F32)],
        compiler_params=params(),
        cost_estimate=cost(
            2 * rows * chans * wide * (seqs + 2 * pair_ch),
            2 * rows * (chans * wide + toks * pair_ch + chans * seqs),
        ),
        name=f"delta_right_{part}",
    )(w_ec, g, a2)


def left_kernel(inv, parts, b_ref, *refs):
    d_refs, o_ref = refs[:parts], refs[parts]
    wide = d_refs[0].shape[1]
    acc = None
    for k in range(parts):
        term = lax.dot_general(
            b_ref[:, k * wide:(k + 1) * wide],
            d_refs[k][...],
            (((1,), (1,)), ((), ())),
            preferred_element_type=F32,
        )
        acc = term if acc is None else acc + term
    o_ref[...] = (acc * inv).astype(BF16)


def left_call(b2, ds, inv, tn):
    seqs = b2.shape[0]
    rows, wide = ds[0].shape
    parts = len(ds)
    return pl.pallas_call(
        functools.partial(left_kernel, inv, parts),
        out_shape=jax.ShapeDtypeStruct((seqs, rows), BF16),
        grid=(rows // tn,),
        in_specs=[pl.BlockSpec((seqs, parts * wide), lambda m: (0, 0))]
        + [pl.BlockSpec((tn, wide), lambda m: (m, 0))] * parts,
        out_specs=pl.BlockSpec((seqs, tn), lambda m: (0, m)),
        compiler_params=params(),
        cost_estimate=cost(2 * seqs * rows * wide * parts, 2 * rows * wide * parts + 4 * seqs * rows),
        name="left",
    )(b2, *ds)


def weight_kernel(chans, *refs):
    o_refs, g_ref, w_ref = refs[:-2], refs[-2], refs[-1]
    ti, toks, pair_ch = g_ref.shape
    per = o_refs[0].shape[1] // toks

    @pl.when(pl.program_id(0) == 0)
    def _():
        w_ref[...] = jnp.zeros_like(w_ref)

    group = 4
    eg = 8 if per % 8 == 0 else 1

    def one(k, carry):
        first = pl.multiple_of(k * group, group)
        right = g_ref[pl.ds(first, group)].reshape(group * toks, pair_ch)
        for h, o_ref in enumerate(o_refs):
            for e0 in range(0, per, eg):
                left = jnp.concatenate(
                    [
                        jnp.concatenate(
                            [
                                o_ref[
                                    pl.ds(pl.multiple_of((first + i) * chans, chans), chans),
                                    e * toks:(e + 1) * toks,
                                ]
                                for i in range(group)
                            ],
                            axis=1,
                        )
                        for e in range(e0, e0 + eg)
                    ],
                    axis=0,
                )
                at = (h * per + e0) * chans
                w_ref[at:at + eg * chans] += jnp.dot(left, right, preferred_element_type=F32)
        return carry

    lax.fori_loop(0, ti // group, one, 0)


def weight_call(outers, g, chans, ti):
    rows, toks, pair_ch = g.shape
    cols = outers[0].shape[1]
    width = cols * len(outers) // toks * chans
    return pl.pallas_call(
        functools.partial(weight_kernel, chans),
        out_shape=jax.ShapeDtypeStruct((width, pair_ch), F32),
        grid=(rows // ti,),
        in_specs=[pl.BlockSpec((ti * chans, cols), lambda m: (m, 0))] * len(outers)
        + [pl.BlockSpec((ti, toks, pair_ch), lambda m: (m, 0, 0))],
        out_specs=pl.BlockSpec((width, pair_ch), lambda m: (0, 0)),
        compiler_params=params(),
        cost_estimate=cost(4 * rows * toks * width * pair_ch, 2 * rows * toks * width),
        name="weight",
    )(*outers, g)


def fused_body(left_factor, right_factor, out_weight, pair_cotangent):
    seqs, chans, rows = left_factor.shape
    toks = right_factor.shape[2]
    pair_ch = out_weight.shape[1]
    inv = 1.0 / (seqs * lax.axis_size("depth"))
    n_col = lax.axis_size("col")
    parts = 4
    eb = chans // parts

    g = lax.all_gather(pair_cotangent, "depth", axis=0, tiled=True)
    a2 = jnp.transpose(left_factor, (0, 2, 1)).reshape(seqs, rows * chans)
    at = jnp.transpose(left_factor, (2, 1, 0)).reshape(rows * chans, seqs)
    b2 = right_factor.reshape(seqs, chans * toks)
    w_ec = jnp.transpose(out_weight.reshape(chans, chans, pair_ch), (1, 0, 2)).reshape(
        chans * chans, pair_ch
    )

    half_cols = b2.shape[1] // 2
    outer_a = outer_call(at, b2, inv, 16 * chans, eb * toks, 0, half_cols)
    g, outer_a = lax.optimization_barrier((g, outer_a))

    ds, rights = [], []
    for k in range(parts):
        d, r = delta_call(w_ec, g, a2, inv, chans, k, eb, 32)
        ds.append(d)
        r, g = lax.optimization_barrier((r, g))
        rights.append(lax.psum_scatter(r, "row", scatter_dimension=0, tiled=True))
    left = left_call(b2, ds, inv, 8 * chans)
    left, at, b2 = lax.optimization_barrier((left, at, b2))
    if n_col == 2:
        half = seqs // 2
        me = lax.axis_index("col")
        mine = lax.dynamic_slice_in_dim(left, me * half, half, 0)
        theirs = lax.dynamic_slice_in_dim(left, (1 - me) * half, half, 0)
        theirs, at, b2 = lax.optimization_barrier((theirs, at, b2))
        got = lax.ppermute(theirs, "col", [(0, 1), (1, 0)])
        left_grad = mine.astype(F32) + got.astype(F32)
    else:
        left_grad = lax.psum_scatter(left, "col", scatter_dimension=0, tiled=True).astype(F32)
    left_grad = jnp.transpose(left_grad.reshape(-1, rows, chans), (0, 2, 1))
    outer_b = outer_call(at, b2, inv, 16 * chans, eb * toks, 1, half_cols)
    weight_acc = weight_call((outer_a, outer_b), g, chans, 8)
    weight_acc = jnp.transpose(weight_acc.reshape(chans, chans, pair_ch), (1, 0, 2)).reshape(
        chans * chans, pair_ch
    )
    axes = ("depth", "row", "col")
    count = lax.axis_size(axes)
    pieces = weight_acc.reshape(count, chans * chans // count, pair_ch)
    pieces = lax.all_to_all(pieces, axes, split_axis=0, concat_axis=0, tiled=True)
    rights = [r.reshape(-1, eb, toks) for r in rights]
    right_grad = jnp.concatenate(rights, axis=1).astype(F32)
    pieces, left_grad, right_grad = lax.optimization_barrier((pieces, left_grad, right_grad))
    weight_grad = jnp.sum(pieces, axis=0)
    return left_grad, right_grad, weight_grad


def plain_body(left_factor, right_factor, out_weight, pair_cotangent):
    seq_total = left_factor.shape[0] * lax.axis_size("depth")
    chans = left_factor.shape[1]
    rows_here = left_factor.shape[2]
    cols_here = right_factor.shape[2]
    width = out_weight.shape[0]
    pair_ch = out_weight.shape[1]
    natural = jnp.einsum("sci,sej->ciej", left_factor, right_factor, preferred_element_type=F32) / seq_total
    outer = jnp.transpose(natural.astype(BF16), (1, 3, 0, 2)).reshape(rows_here * cols_here, width)
    piece = lax.all_gather(pair_cotangent, "depth", axis=0, tiled=True)
    grad_two = piece.reshape(rows_here * cols_here, pair_ch)
    delta = jnp.dot(grad_two, out_weight.T, preferred_element_type=F32).astype(BF16)
    weight_acc = jnp.dot(outer.T, grad_two, preferred_element_type=F32)
    delta_four = delta.reshape(rows_here, cols_here, chans, chans)
    left_part = jnp.einsum("ijce,sej->sci", delta_four, right_factor, preferred_element_type=F32) / seq_total
    right_part = jnp.einsum("ijce,sci->sej", delta_four, left_factor, preferred_element_type=F32) / seq_total
    left_grad = lax.psum_scatter(left_part, "col", scatter_dimension=0, tiled=True)
    right_grad = lax.psum_scatter(right_part, "row", scatter_dimension=0, tiled=True)
    middle = lax.psum_scatter(weight_acc, ("depth", "row"), scatter_dimension=0, tiled=True)
    weight_grad = lax.psum_scatter(middle, "col", scatter_dimension=0, tiled=True)
    return left_grad, right_grad, weight_grad


def body(left_factor, right_factor, out_weight, pair_cotangent):
    seqs, chans, rows = left_factor.shape
    toks = right_factor.shape[2]
    fits = toks % 128 == 0 and toks <= 256 and rows % 32 == 0 and chans == 32 and seqs <= 512
    run = fused_body if fits else plain_body
    return run(left_factor, right_factor, out_weight, pair_cotangent)


def solution(mesh):
    return jax.shard_map(
        body,
        mesh=mesh,
        in_specs=(
            P("depth", None, "row"),
            P("depth", None, "col"),
            P(),
            P(("row", "depth"), "col", None),
        ),
        out_specs=(
            P(("depth", "col"), None, "row"),
            P(("depth", "row"), None, "col"),
            P(("depth", "row", "col"), None),
        ),
        check_vma=False,
    )
```
